32 devices in a mesh: gx: 4 (over y, x), gy: 8 (over z, core).
Axes of the slice: x: 2, y: 2, z: 4, core: 2. Of those that a mesh axis runs over, the one named last changes fastest.
Arguments:
- thermal_field: bfloat16 [384, 384, 128], P('gx', 'gy'), may hold values from -6 to 6
- probe_range_east: bfloat16 [384, 128], P('gx'), may hold values from -0.3125 to 0.3125
- probe_range_north: bfloat16 [384, 128], P('gy'), may hold values from -0.3125 to 0.3125
- probe_range_upward: bfloat16 [128, 128], replicated, may hold values from -0.5 to 0.5
- gauss_kernel_east: bfloat16 [384, 384], replicated, may hold values from -0.3125 to 0.3125
- gauss_kernel_north: bfloat16 [384, 384], replicated, may hold values from -0.3125 to 0.3125
- gauss_kernel_upward: bfloat16 [384, 128], replicated, may hold values from -0.5 to 0.5
Outputs:
- factor_x: float32 [384, 128], P('gx')
- factor_y: float32 [384, 128], P('gy')
- factor_z: float32 [128, 128], replicated
- core_sketch: float32 [384, 384, 384], P('gx', None, 'gy')
The draws below stay inside these ranges and needn't reach their ends.
All inputs are finite; a program needn't handle non-finite values.
Results may differ from the reference program's by a relative error of at most 0.0029.
Values may be sent and summed in bfloat16 or wider, within the bound.
A program may use at most 64 MiB of HBM per device.

```python
import jax
import jax.numpy as jnp
from jax import lax

POINTS_IN_SHARD = 96
SHEET_HEIGHT_UP = 128
K = 128
S = 384
MESH_WIDTH_EAST = 384
MESH_WIDTH_NORTH = 384
N_GX = 4


def steps_of(stream_key, dims, shards, smallest, largest):
    gain = 1.0
    for position, shards_of in shards:
        draws = jax.random.uniform(jax.random.fold_in(jax.random.fold_in(stream_key, 6), position), (shards_of,), jnp.float32, smallest / len(shards), largest / len(shards))
        gain = gain * jnp.repeat(jnp.exp(draws), dims[position] // shards_of).reshape((-1,) + (1,) * (len(dims) - 1 - position))
    return gain


def gaussian(stream_key, shape, scale, reach, split=(), kind=jnp.bfloat16):
    values = scale * jax.random.normal(stream_key, shape, jnp.float32)
    if split:
        values = values * steps_of(stream_key, shape, split, -0.22, 0.18)
    return jnp.clip(values, -reach, reach).astype(kind)


def setup_inputs(seed: int = 0) -> dict:
    streams_of = jax.random.split(jax.random.key(seed), 8)
    return {
        "thermal_field": gaussian(streams_of[0], (MESH_WIDTH_EAST, MESH_WIDTH_NORTH, SHEET_HEIGHT_UP), 1.0, 6.0, ((0, 4), (1, 8))),
        "probe_range_east": gaussian(streams_of[1], (MESH_WIDTH_EAST, K), MESH_WIDTH_EAST ** -0.5, 0.3125, ((0, 4),)),
        "probe_range_north": gaussian(streams_of[2], (MESH_WIDTH_NORTH, K), MESH_WIDTH_NORTH ** -0.5, 0.3125, ((0, 8),)),
        "probe_range_upward": gaussian(streams_of[3], (SHEET_HEIGHT_UP, K), SHEET_HEIGHT_UP ** -0.5, 0.5),
        "gauss_kernel_east": gaussian(streams_of[4], (S, MESH_WIDTH_EAST), MESH_WIDTH_EAST ** -0.5, 0.3125),
        "gauss_kernel_north": gaussian(streams_of[5], (S, MESH_WIDTH_NORTH), MESH_WIDTH_NORTH ** -0.5, 0.3125),
        "gauss_kernel_upward": gaussian(streams_of[6], (S, SHEET_HEIGHT_UP), SHEET_HEIGHT_UP ** -0.5, 0.5),
    }


def reference(thermal_field, probe_range_east, probe_range_north, probe_range_upward, gauss_kernel_east, gauss_kernel_north, gauss_kernel_upward):
    highest = lax.Precision.HIGHEST
    width = probe_range_upward.shape[1]
    along_x = probe_range_east.astype(jnp.float32)
    along_y = probe_range_north.astype(jnp.float32)

    def block(carry, index):
        part_y, part_z = carry
        opening_offset = (index * POINTS_IN_SHARD).astype(jnp.int32)
        point_total = lax.dynamic_slice_in_dim(thermal_field, opening_offset, POINTS_IN_SHARD, 0)
        rows_x = lax.dynamic_slice_in_dim(along_x, opening_offset, POINTS_IN_SHARD, 0)
        unrolled_tensor = point_total.reshape(POINTS_IN_SHARD * MESH_WIDTH_NORTH, SHEET_HEIGHT_UP)
        weighted = jnp.dot(unrolled_tensor, probe_range_upward, preferred_element_type=jnp.float32).reshape(POINTS_IN_SHARD, MESH_WIDTH_NORTH, width)
        factor_rows = jnp.sum(weighted * along_y[None, :, :], axis=1)
        part_y = part_y + jnp.sum(weighted * rows_x[:, None, :], axis=0)
        khatri = (rows_x[:, None, :] * along_y[None, :, :]).astype(jnp.bfloat16).reshape(POINTS_IN_SHARD * MESH_WIDTH_NORTH, width)
        part_z = part_z + jnp.dot(unrolled_tensor.T, khatri, preferred_element_type=jnp.float32)
        return (part_y, part_z), factor_rows

    start_carry = (jnp.zeros((MESH_WIDTH_NORTH, width), jnp.float32), jnp.zeros((SHEET_HEIGHT_UP, width), jnp.float32))
    (factor_y, factor_z), blocks = lax.scan(block, start_carry, jnp.arange(N_GX, dtype=jnp.int32))
    factor_x = blocks.reshape(MESH_WIDTH_EAST, width)

    leading_offset = jnp.dot(gauss_kernel_east, thermal_field.reshape(MESH_WIDTH_EAST, MESH_WIDTH_NORTH * SHEET_HEIGHT_UP), preferred_element_type=jnp.float32)
    leading_offset = leading_offset.reshape(S, MESH_WIDTH_NORTH, SHEET_HEIGHT_UP)
    second = jnp.einsum("ajl,bj->abl", leading_offset, gauss_kernel_north.astype(jnp.float32), precision=highest)
    core_sketch = jnp.einsum("abl,cl->abc", second, gauss_kernel_upward.astype(jnp.float32), precision=highest)
    return factor_x, factor_y, factor_z, core_sketch
```

```python
import jax
import jax.numpy as jnp
from jax import lax
from jax.sharding import PartitionSpec as P


def per_device(
    thermal_field,
    probe_range_east,
    probe_range_north,
    probe_range_upward,
    gauss_kernel_east,
    gauss_kernel_north,
    gauss_kernel_upward,
):
    line_tally, span_breadth, height_tally = thermal_field.shape
    width = probe_range_upward.shape[1]
    unrolled_tensor = thermal_field.reshape(line_tally * span_breadth, height_tally)
    weighted = jnp.dot(
        unrolled_tensor, probe_range_upward, preferred_element_type=jnp.float32
    ).reshape(line_tally, span_breadth, width)
    along_x = probe_range_east.astype(jnp.float32)
    along_y = probe_range_north.astype(jnp.float32)
    part_x = jnp.sum(weighted * along_y[None, :, :], axis=1)
    part_y = jnp.sum(weighted * along_x[:, None, :], axis=0)
    khatri = (
        (along_x[:, None, :] * along_y[None, :, :])
        .astype(jnp.bfloat16)
        .reshape(line_tally * span_breadth, width)
    )
    part_z = lax.dot_general(
        unrolled_tensor, khatri, (((0,), (0,)), ((), ())), preferred_element_type=jnp.float32
    )
    factor_x = lax.psum(part_x, "gy")
    factor_y = lax.psum(part_y, "gx")
    factor_z = lax.psum(part_z, ("gx", "gy"))
    bf = jnp.bfloat16
    mixed = jnp.einsum(
        "ijl,ai->ajl",
        lax.all_to_all(thermal_field, "gx", split_axis=2, concat_axis=0, tiled=True),
        gauss_kernel_east,
        preferred_element_type=jnp.float32,
    ).astype(bf)
    mixed = jnp.einsum(
        "ajl,cl->ajc",
        lax.all_to_all(mixed, "gx", split_axis=0, concat_axis=2, tiled=True),
        gauss_kernel_upward,
        preferred_element_type=jnp.float32,
    ).astype(bf)
    core_sketch = jnp.einsum(
        "ajc,bj->abc",
        lax.all_to_all(mixed, "gy", split_axis=2, concat_axis=1, tiled=True),
        gauss_kernel_north,
        preferred_element_type=jnp.float32,
    )
    return (factor_x, factor_y, factor_z, core_sketch)


def solution(mesh):
    in_specs = (P("gx", "gy", None), P("gx", None), P("gy", None), P(), P(), P(), P())
    out_specs = (P("gx", None), P("gy", None), P(), P("gx", None, "gy"))
    return jax.shard_map(
        per_device, mesh=mesh, in_specs=in_specs, out_specs=out_specs, check_vma=False
    )
```

```python
import functools

import jax
import jax.numpy as jnp
from jax import lax
from jax.experimental import pallas as pl
from jax.experimental.pallas import tpu as pltpu
from jax.sharding import PartitionSpec as P

MESH = pl.DeviceIdType.MESH
VMEM = pl.BlockSpec(memory_space=pltpu.VMEM)
ANY = pl.BlockSpec(memory_space=pl.ANY)
BF = jnp.bfloat16
F32 = jnp.float32


def remote(src, dst, send, recv, where):
    copy = pltpu.make_async_remote_copy(
        src_ref=src, dst_ref=dst, send_sem=send, recv_sem=recv, device_id=where, device_id_type=MESH
    )
    copy.start()
    return copy


def mix_x_kernel(n, chunks, t_ref, g_ref, w_ref, x_buf, y_buf, s1, r1, s2, r2, ls):
    gx, gy = lax.axis_index("gx"), lax.axis_index("gy")
    rows = t_ref.shape[0]
    a_rows = y_buf.shape[2]
    wide = t_ref.shape[1] // n
    part = wide // chunks
    barrier = pltpu.get_barrier_semaphore()
    for d in range(1, n):
        pl.semaphore_signal(barrier, inc=1, device_id=(lax.rem(gx + d, n), gy), device_id_type=MESH)
    pl.semaphore_wait(barrier, n - 1)

    first, second, local = [], [], []
    for m in range(chunks):
        for d in range(1, n):
            to = lax.rem(gx + d, n)
            lanes = pl.ds(pl.multiple_of(to * wide + m * part, 128), part)
            first.append(
                remote(t_ref.at[:, lanes], x_buf.at[m, gx], s1.at[m, d], r1.at[m, d], (to, gy))
            )
        lanes = pl.ds(pl.multiple_of(gx * wide + m * part, 128), part)
        own = pltpu.make_async_copy(t_ref.at[:, lanes], x_buf.at[m, gx], ls.at[m, 0])
        own.start()
        local.append(own)
    for m in range(chunks):
        local[m].wait()
        for d in range(1, n):
            first[m * (n - 1) + d - 1].wait()
        block = x_buf[m].reshape(n * rows, part)
        lanes = pl.ds(pl.multiple_of(gx * wide + m * part, 128), part)
        for d in range(1, n + 1):
            to = lax.rem(gx + d, n)
            y_buf[m, d - 1] = jnp.dot(g_ref[to], block, preferred_element_type=F32).astype(BF)
            if d < n:
                second.append(
                    remote(
                        y_buf.at[m, d - 1], w_ref.at[:, lanes], s2.at[m, d], r2.at[m, d], (to, gy)
                    )
                )
            else:
                own = pltpu.make_async_copy(y_buf.at[m, d - 1], w_ref.at[:, lanes], ls.at[m, 1])
                own.start()
                second.append(own)
    for copy in second:
        copy.wait()


def mix_x(field, gauss, n, a_rows):
    rows, lanes = field.shape
    wide = lanes // n
    chunks = 3 if wide % 384 == 0 else 1
    dma = lambda *shape: pltpu.SemaphoreType.DMA(shape)
    return pl.pallas_call(
        functools.partial(mix_x_kernel, n, chunks),
        out_shape=jax.ShapeDtypeStruct((a_rows, lanes), BF),
        in_specs=[VMEM, VMEM],
        out_specs=VMEM,
        scratch_shapes=[
            pltpu.VMEM((chunks, n, rows, wide // chunks), BF),
            pltpu.VMEM((chunks, n, a_rows, wide // chunks), BF),
            dma(chunks, n), dma(chunks, n), dma(chunks, n), dma(chunks, n), dma(chunks, 2),
        ],
        compiler_params=pltpu.CompilerParams(collective_id=0, has_side_effects=True),
    )(field, gauss)


def exchange_kernel(
    nx, ny, batches, per_c, w_ref, gt_ref, mask_ref, q_ref, py_ref,
    r_ref, qo_ref, pyo_ref,
    u_buf, q_in, q_all, y_in, z_in, z_own,
    us, ur, ul, qs, qr, ys, yr, zs, zr, gs, gr,
):
    gx, gy = lax.axis_index("gx"), lax.axis_index("gy")
    span = u_buf.shape[3]
    per = u_buf.shape[2]
    lanes = u_buf.shape[4]
    a_in = mask_ref.shape[0]
    deep = gt_ref.shape[1]
    x_rows = q_ref.shape[1] - z_in.shape[1]
    barrier = pltpu.get_barrier_semaphore()
    for d in range(1, ny):
        pl.semaphore_signal(barrier, inc=1, device_id=(gx, lax.rem(gy + d, ny)), device_id_type=MESH)
    for d in range(1, nx):
        pl.semaphore_signal(barrier, inc=1, device_id=(lax.rem(gx + d, nx), gy), device_id_type=MESH)
    pl.semaphore_wait(barrier, nx + ny - 2)

    small, ysmall, big = [], [], []
    for d in range(1, ny):
        to = lax.rem(gy + d, ny)
        small.append(remote(q_ref.at[to], q_in.at[d], qs.at[d], qr.at[d], (gx, to)))
    for d in range(1, nx):
        to = lax.rem(gx + d, nx)
        ysmall.append(remote(py_ref, y_in.at[d], ys.at[d], yr.at[d], (to, gy)))

    rows_b = per * span
    for b in range(batches):
        for d in range(1, ny + 1):
            to = lax.rem(gy + d, ny)
            for tile in range(lanes // 128):
                low = min(tile * 128 // per_c, a_in - 1)
                high = min((tile * 128 + 127) // per_c, a_in - 1)
                here = slice(tile * 128, tile * 128 + 128)
                weights = jnp.concatenate(
                    [gt_ref[to, :, here] * mask_ref[k : k + 1, here] for k in range(low, high + 1)], axis=0
                )
                left = w_ref[b * rows_b : (b + 1) * rows_b, low * deep : (high + 1) * deep]
                got = jnp.dot(left, weights, preferred_element_type=F32).astype(BF)
                u_buf[b, d - 1, :, :, here] = got.reshape(per, span, 128)
            target = r_ref.at[pl.ds(b * per, per), pl.ds(pl.multiple_of(gy * span, span), span), :]
            if d < ny:
                big.append(remote(u_buf.at[b, d - 1], target, us.at[b, d], ur.at[b, d], (gx, to)))
            else:
                own = pltpu.make_async_copy(u_buf.at[b, d - 1], target, ul.at[b])
                own.start()
                big.append(own)
        if b == 0:
            for copy in small:
                copy.wait()
            total = q_ref[gy]
            for d in range(1, ny):
                total = total + q_in[d]
            z_own[...] = total[x_rows:]
            zsmall = []
            for d in range(1, nx):
                to = lax.rem(gx + d, nx)
                zsmall.append(remote(z_own, z_in.at[d], zs.at[d], zr.at[d], (to, gy)))
            for copy in ysmall:
                copy.wait()
            y_in[0] = py_ref[...]
            y_total = jnp.zeros(py_ref.shape, F32)
            for g in range(nx):
                y_total = y_total + y_in[lax.rem(gx - g + nx, nx)]
            pyo_ref[...] = y_total
    for copy in zsmall:
        copy.wait()
    z_in[0] = z_own[...]
    z_total = jnp.zeros(z_own.shape, F32)
    for g in range(nx):
        z_total = z_total + z_in[lax.rem(gx - g + nx, nx)]
    q_all[gy, :x_rows] = total[:x_rows]
    q_all[gy, x_rows:] = z_total
    gathers = []
    for d in range(1, ny):
        to = lax.rem(gy + d, ny)
        gathers.append(remote(q_all.at[gy], q_all.at[gy], gs.at[d], gr.at[d], (gx, to)))
    for copy in gathers:
        copy.wait()
    qo_ref[...] = q_all[...]
    for copy in big:
        copy.wait()


def exchange(w, gt, mask, q, py, nx, ny, groups, span, per_c):
    batches = 3 if groups % 3 == 0 else 1
    per = groups // batches
    lanes = gt.shape[2]
    z_rows = gt.shape[1] // ny
    dma = lambda *shape: pltpu.SemaphoreType.DMA(shape)
    vm = pltpu.VMEM
    return pl.pallas_call(
        functools.partial(exchange_kernel, nx, ny, batches, per_c),
        out_shape=(
            jax.ShapeDtypeStruct((groups, ny * span, lanes), BF),
            jax.ShapeDtypeStruct(q.shape, F32),
            jax.ShapeDtypeStruct(py.shape, F32),
        ),
        in_specs=[VMEM] * 5,
        out_specs=(ANY, VMEM, VMEM),
        scratch_shapes=[
            vm((batches, ny, per, span, lanes), BF),
            vm(q.shape, F32), vm(q.shape, F32), vm((nx,) + py.shape, F32),
            vm((nx, z_rows, q.shape[2]), F32), vm((z_rows, q.shape[2]), F32),
            dma(batches, ny), dma(batches, ny), dma(batches),
            dma(ny), dma(ny), dma(nx), dma(nx), dma(nx), dma(nx), dma(ny), dma(ny),
        ],
        compiler_params=pltpu.CompilerParams(collective_id=1, has_side_effects=True),
    )(w, gt, mask, q, py)


def mix_y_kernel(r_ref, g_ref, o_ref):
    o_ref[0] = lax.dot_general(
        r_ref[0], g_ref[...], (((0,), (0,)), ((), ())), preferred_element_type=F32
    )


def mix_y(r, g):
    groups, deep, lanes = r.shape
    out = g.shape[1]
    return pl.pallas_call(
        mix_y_kernel,
        grid=(groups,),
        out_shape=jax.ShapeDtypeStruct((groups, lanes, out), F32),
        in_specs=[
            pl.BlockSpec((1, deep, lanes), lambda i: (i, 0, 0)),
            pl.BlockSpec((deep, out), lambda i: (0, 0)),
        ],
        out_specs=pl.BlockSpec((1, lanes, out), lambda i: (i, 0, 0)),
    )(r, g)


def per_device(
    nx, ny,
    thermal_field,
    probe_range_east,
    probe_range_north,
    probe_range_upward,
    gauss_kernel_east,
    gauss_kernel_north,
    gauss_kernel_upward,
):
    rows, span, deep = thermal_field.shape
    width = probe_range_upward.shape[1]
    a_rows = gauss_kernel_east.shape[0] // nx
    per_c = gauss_kernel_upward.shape[0] // ny
    a_in = 8 if a_rows % 8 == 0 and 8 * per_c % 128 == 0 else a_rows
    groups = a_rows // a_in
    used = a_in * per_c
    lanes = -(-used // 128) * 128

    w = mix_x(
        thermal_field.reshape(rows, span * deep),
        gauss_kernel_east.reshape(nx, a_rows, -1),
        nx,
        a_rows,
    )
    w = w.reshape(groups, a_in, span, deep).transpose(0, 2, 1, 3).reshape(groups * span, a_in * deep)

    unrolled = thermal_field.reshape(rows * span, deep)
    weighted = jnp.dot(unrolled, probe_range_upward, preferred_element_type=F32)
    weighted = weighted.reshape(rows, span, width)
    along_x = probe_range_east.astype(F32)
    along_y = probe_range_north.astype(F32)
    part_x = jnp.sum(weighted * along_y[None, :, :], axis=1)
    part_y = jnp.sum(weighted * along_x[:, None, :], axis=0)
    khatri = (along_x[:, None, :] * along_y[None, :, :]).astype(BF).reshape(rows * span, width)
    part_z = lax.dot_general(
        unrolled, khatri, (((0,), (0,)), ((), ())), preferred_element_type=F32
    )
    q = jnp.concatenate(
        [part_x.reshape(ny, rows // ny, width), part_z.reshape(ny, deep // ny, width)], axis=1
    )

    gt = gauss_kernel_upward.reshape(ny, per_c, deep).transpose(0, 2, 1)
    gt = jnp.pad(jnp.tile(gt, (1, 1, a_in)), ((0, 0), (0, 0), (0, lanes - used)))
    mask = (
        lax.broadcasted_iota(jnp.int32, (a_in, lanes), 1) // per_c
        == lax.broadcasted_iota(jnp.int32, (a_in, lanes), 0)
    ).astype(BF)
    r, q_sum, factor_y = exchange(w, gt, mask, q, part_y, nx, ny, groups, span, per_c)
    factor_x = q_sum[:, : rows // ny].reshape(rows, width)
    factor_z = q_sum[:, rows // ny :].reshape(deep, width)

    core = mix_y(r, gauss_kernel_north.T)
    core = core[:, :used].reshape(a_rows, per_c, -1).transpose(0, 2, 1)
    return (factor_x, factor_y, factor_z, core)


def solution(mesh):
    in_specs = (P("gx", "gy", None), P("gx", None), P("gy", None), P(), P(), P(), P())
    out_specs = (P("gx", None), P("gy", None), P(), P("gx", None, "gy"))
    body = functools.partial(per_device, mesh.shape["gx"], mesh.shape["gy"])
    return jax.shard_map(
        body, mesh=mesh, in_specs=in_specs, out_specs=out_specs, check_vma=False
    )
```

```python
import functools

import jax
import jax.numpy as jnp
from jax import lax
from jax.experimental import pallas as pl
from jax.experimental.pallas import tpu as pltpu
from jax.sharding import PartitionSpec as P

MESH = pl.DeviceIdType.MESH
VMEM = pl.BlockSpec(memory_space=pltpu.VMEM)
ANY = pl.BlockSpec(memory_space=pl.ANY)
BF = jnp.bfloat16
F32 = jnp.float32


def remote(src, dst, send, recv, where):
    copy = pltpu.make_async_remote_copy(
        src_ref=src, dst_ref=dst, send_sem=send, recv_sem=recv, device_id=where, device_id_type=MESH
    )
    copy.start()
    return copy


def mix_x_kernel(n, chunks, t_ref, g_ref, w_ref, x_buf, y_buf, s1, r1, s2, r2, ls):
    gx, gy = lax.axis_index("gx"), lax.axis_index("gy")
    rows = t_ref.shape[0]
    a_rows = y_buf.shape[2]
    wide = t_ref.shape[1] // n
    part = wide // chunks
    barrier = pltpu.get_barrier_semaphore()
    for d in range(1, n):
        pl.semaphore_signal(barrier, inc=1, device_id=(lax.rem(gx + d, n), gy), device_id_type=MESH)
    pl.semaphore_wait(barrier, n - 1)

    first, second, local = [], [], []
    for m in range(chunks):
        for d in range(1, n):
            to = lax.rem(gx + d, n)
            lanes = pl.ds(pl.multiple_of(to * wide + m * part, 128), part)
            first.append(
                remote(t_ref.at[:, lanes], x_buf.at[m, gx], s1.at[m, d], r1.at[m, d], (to, gy))
            )
        lanes = pl.ds(pl.multiple_of(gx * wide + m * part, 128), part)
        own = pltpu.make_async_copy(t_ref.at[:, lanes], x_buf.at[m, gx], ls.at[m, 0])
        own.start()
        local.append(own)
    for m in range(chunks):
        local[m].wait()
        for d in range(1, n):
            first[m * (n - 1) + d - 1].wait()
        block = x_buf[m].reshape(n * rows, part)
        lanes = pl.ds(pl.multiple_of(gx * wide + m * part, 128), part)
        for d in range(1, n + 1):
            to = lax.rem(gx + d, n)
            y_buf[m, d - 1] = jnp.dot(g_ref[to], block, preferred_element_type=F32).astype(BF)
            if d < n:
                second.append(
                    remote(
                        y_buf.at[m, d - 1], w_ref.at[:, lanes], s2.at[m, d], r2.at[m, d], (to, gy)
                    )
                )
            else:
                own = pltpu.make_async_copy(y_buf.at[m, d - 1], w_ref.at[:, lanes], ls.at[m, 1])
                own.start()
                second.append(own)
    for copy in second:
        copy.wait()


def mix_x(field, gauss, n, a_rows):
    rows, lanes = field.shape
    wide = lanes // n
    chunks = 3 if wide % 384 == 0 else 1
    dma = lambda *shape: pltpu.SemaphoreType.DMA(shape)
    return pl.pallas_call(
        functools.partial(mix_x_kernel, n, chunks),
        out_shape=jax.ShapeDtypeStruct((a_rows, lanes), BF),
        in_specs=[VMEM, VMEM],
        out_specs=VMEM,
        scratch_shapes=[
            pltpu.VMEM((chunks, n, rows, wide // chunks), BF),
            pltpu.VMEM((chunks, n, a_rows, wide // chunks), BF),
            dma(chunks, n), dma(chunks, n), dma(chunks, n), dma(chunks, n), dma(chunks, 2),
        ],
        compiler_params=pltpu.CompilerParams(collective_id=0, has_side_effects=True),
    )(field, gauss)


def exchange_kernel(
    nx, ny, batches, per_c, w_ref, gt_ref, mask_ref, q_ref, py_ref,
    r_ref, qo_ref, pyo_ref,
    u_buf, q_in, q_all, y_in, z_in, z_own,
    us, ur, ul, qs, qr, ys, yr, zs, zr, gs, gr,
):
    gx, gy = lax.axis_index("gx"), lax.axis_index("gy")
    span = u_buf.shape[3]
    per = u_buf.shape[2]
    lanes = u_buf.shape[4]
    a_in = mask_ref.shape[0]
    deep = gt_ref.shape[1]
    x_rows = q_ref.shape[1] - z_in.shape[1]
    barrier = pltpu.get_barrier_semaphore()
    for d in range(1, ny):
        pl.semaphore_signal(barrier, inc=1, device_id=(gx, lax.rem(gy + d, ny)), device_id_type=MESH)
    for d in range(1, nx):
        pl.semaphore_signal(barrier, inc=1, device_id=(lax.rem(gx + d, nx), gy), device_id_type=MESH)
    pl.semaphore_wait(barrier, nx + ny - 2)

    small, ysmall, big = [], [], []
    for d in range(1, ny):
        to = lax.rem(gy + d, ny)
        small.append(remote(q_ref.at[to], q_in.at[d], qs.at[d], qr.at[d], (gx, to)))
    for d in range(1, nx):
        to = lax.rem(gx + d, nx)
        ysmall.append(remote(py_ref, y_in.at[d], ys.at[d], yr.at[d], (to, gy)))

    rows_b = per * span
    for b in range(batches):
        for d in range(1, ny + 1):
            to = lax.rem(gy + d, ny)
            for tile in range(lanes // 128):
                low = min(tile * 128 // per_c, a_in - 1)
                high = min((tile * 128 + 127) // per_c, a_in - 1)
                here = slice(tile * 128, tile * 128 + 128)
                weights = jnp.concatenate(
                    [gt_ref[to, :, here] * mask_ref[k : k + 1, here] for k in range(low, high + 1)], axis=0
                )
                left = w_ref[b * rows_b : (b + 1) * rows_b, low * deep : (high + 1) * deep]
                got = jnp.dot(left, weights, preferred_element_type=F32).astype(BF)
                u_buf[b, d - 1, :, :, here] = got.reshape(per, span, 128)
            target = r_ref.at[pl.ds(b * per, per), pl.ds(pl.multiple_of(gy * span, span), span), :]
            if d < ny:
                big.append(remote(u_buf.at[b, d - 1], target, us.at[b, d], ur.at[b, d], (gx, to)))
            else:
                own = pltpu.make_async_copy(u_buf.at[b, d - 1], target, ul.at[b])
                own.start()
                big.append(own)
        if b == 0:
            for copy in small:
                copy.wait()
            total = q_ref[gy]
            for d in range(1, ny):
                total = total + q_in[d]
            z_own[...] = total[x_rows:]
            zsmall = []
            for d in range(1, nx):
                to = lax.rem(gx + d, nx)
                zsmall.append(remote(z_own, z_in.at[d], zs.at[d], zr.at[d], (to, gy)))
            for copy in ysmall:
                copy.wait()
            y_in[0] = py_ref[...]
            y_total = jnp.zeros(py_ref.shape, F32)
            for g in range(nx):
                y_total = y_total + y_in[lax.rem(gx - g + nx, nx)]
            pyo_ref[...] = y_total
    for copy in zsmall:
        copy.wait()
    z_in[0] = z_own[...]
    z_total = jnp.zeros(z_own.shape, F32)
    for g in range(nx):
        z_total = z_total + z_in[lax.rem(gx - g + nx, nx)]
    q_all[gy, :x_rows] = total[:x_rows]
    q_all[gy, x_rows:] = z_total
    gathers = []
    for d in range(1, ny):
        to = lax.rem(gy + d, ny)
        gathers.append(remote(q_all.at[gy], q_all.at[gy], gs.at[d], gr.at[d], (gx, to)))
    for copy in gathers:
        copy.wait()
    qo_ref[...] = q_all[...]
    for copy in big:
        copy.wait()


def line_kernel(
    nx, ny, batches, per_c, w_ref, gt_ref, mask_ref, q_ref, py_ref,
    r_ref, qo_ref, pyo_ref,
    w_in, u_buf, wt, q_in, q_all, y_in, z_in, z_own,
    ws, wr, us, ur, ul, qs, qr, ys, yr, zs, zr, gs, gr,
):
    gx, gy = lax.axis_index("gx"), lax.axis_index("gy")
    spot, core = gy // 2, gy % 2
    last = ny // 2 - 1
    middle = jnp.logical_and(spot > 0, spot < last)
    left_half = spot * 2 < last
    end = jnp.where(left_half, 0, last)
    near = jnp.where(left_half, 1, last - 1)
    _, _, _, per, span, lanes = u_buf.shape
    a_in = mask_ref.shape[0]
    deep = gt_ref.shape[1]
    x_rows = q_ref.shape[1] - z_in.shape[1]
    rows_b = per * span
    spots = (end, last - spot, last - end, spot)
    goals = (gy, 2 * spot + 1 - core, 2 * end, 2 * end + 1)
    barrier = pltpu.get_barrier_semaphore()
    for d in range(1, ny):
        pl.semaphore_signal(barrier, inc=1, device_id=(gx, lax.rem(gy + d, ny)), device_id_type=MESH)
    for d in range(1, nx):
        pl.semaphore_signal(barrier, inc=1, device_id=(lax.rem(gx + d, nx), gy), device_id_type=MESH)
    pl.semaphore_wait(barrier, nx + ny - 2)

    small, ysmall = [], []
    for d in range(1, ny):
        to = lax.rem(gy + d, ny)
        small.append(remote(q_ref.at[to], q_in.at[d], qs.at[d], qr.at[d], (gx, to)))
    for d in range(1, nx):
        to = lax.rem(gx + d, nx)
        ysmall.append(remote(py_ref, y_in.at[d], ys.at[d], yr.at[d], (to, gy)))

    def raw(src, slot, b, to_spot):
        return pltpu.make_async_remote_copy(
            src_ref=src, dst_ref=w_in.at[slot, b], send_sem=ws.at[slot, b], recv_sem=wr.at[slot, b],
            device_id=(gx, 2 * to_spot + core), device_id_type=MESH,
        )

    def rows_of(b):
        return w_ref.at[pl.ds(b * rows_b, rows_b), :]

    def place(b, origin):
        return r_ref.at[pl.ds(b * per, per), pl.ds(pl.multiple_of(origin * span, span), span), :]

    def block(kind, slot, b):
        source = 2 * spots[slot] + core
        if kind == 0:
            return pltpu.make_async_copy(u_buf.at[kind, slot, b], place(b, source), ul.at[slot, b])
        return pltpu.make_async_remote_copy(
            src_ref=u_buf.at[kind, slot, b], dst_ref=place(b, source),
            send_sem=us.at[kind, slot, b], recv_sem=ur.at[b, spots[slot], core],
            device_id=(gx, goals[kind]), device_id_type=MESH,
        )

    def arrived(b, at, side):
        pltpu.make_async_remote_copy(
            src_ref=u_buf.at[0, 0, b], dst_ref=place(b, 2 * at + side),
            send_sem=us.at[1, 0, b], recv_sem=ur.at[b, at, side],
            device_id=(gx, goals[1]), device_id_type=MESH,
        ).wait_recv()

    pieces, base = [], 0
    for tile in range(lanes // 128):
        low = min(tile * 128 // per_c, a_in - 1)
        high = min((tile * 128 + 127) // per_c, a_in - 1)
        pieces.append((tile, low, high, base))
        base += (high + 1 - low) * deep

    def weigh(kind):
        for tile, low, high, at in pieces:
            here = slice(tile * 128, tile * 128 + 128)
            for k in range(low, high + 1):
                wt[kind, at + (k - low) * deep : at + (k - low + 1) * deep] = (
                    gt_ref[goals[kind], :, here] * mask_ref[k : k + 1, here]
                )

    def mix(kind, slot, b, left):
        for tile, low, high, at in pieces:
            got = jnp.dot(
                left[:, low * deep : (high + 1) * deep],
                wt[kind, at : at + (high + 1 - low) * deep],
                preferred_element_type=F32,
            ).astype(BF)
            u_buf[kind, slot, b, :, :, tile * 128 : tile * 128 + 128] = got.reshape(per, span, 128)

    def own_blocks(kind):
        weigh(kind)
        for b in range(batches):
            mix(kind, 3, b, rows_of(b))
            block(kind, 3, b).start()

    @pl.when(middle)
    def _():
        for b in range(batches):
            raw(rows_of(b), 1, b, last - spot).start()
        for kind in (2, 3):
            own_blocks(kind)

    @pl.when(jnp.logical_not(middle))
    def _():
        for b in range(batches):
            raw(rows_of(b), 0, b, near).start()

    for kind in (1, 0):
        own_blocks(kind)

    for copy in small:
        copy.wait()
    total = q_ref[gy]
    for d in range(1, ny):
        total = total + q_in[d]
    z_own[...] = total[x_rows:]
    zsmall = []
    for d in range(1, nx):
        to = lax.rem(gx + d, nx)
        zsmall.append(remote(z_own, z_in.at[d], zs.at[d], zr.at[d], (to, gy)))
    for copy in ysmall:
        copy.wait()
    y_in[0] = py_ref[...]
    y_total = jnp.zeros(py_ref.shape, F32)
    for g in range(nx):
        y_total = y_total + y_in[lax.rem(gx - g + nx, nx)]
    pyo_ref[...] = y_total
    for copy in zsmall:
        copy.wait()
    z_in[0] = z_own[...]
    z_total = jnp.zeros(z_own.shape, F32)
    for g in range(nx):
        z_total = z_total + z_in[lax.rem(gx - g + nx, nx)]
    q_all[gy, :x_rows] = total[:x_rows]
    q_all[gy, x_rows:] = z_total
    gathers = []
    for d in range(1, ny):
        to = lax.rem(gy + d, ny)
        gathers.append(remote(q_all.at[gy], q_all.at[gy], gs.at[d], gr.at[d], (gx, to)))

    @pl.when(middle)
    def _():
        for b in range(batches):
            raw(rows_of(b), 0, b, near).wait_recv()
            raw(w_in.at[0, b], 2, b, last - spot).start()
            raw(rows_of(b), 1, b, last - spot).wait_recv()
            for kind, slot in ((2, 1), (3, 1), (1, 1), (1, 0), (0, 1), (0, 0)):
                mix(kind, slot, b, w_in.at[slot, b])
                block(kind, slot, b).start()
        for b in range(batches):
            raw(w_in.at[0, b], 2, b, last - spot).wait_recv()
            for kind in (2, 3, 1, 0):
                mix(kind, 2, b, w_in.at[2, b])
                block(kind, 2, b).start()
        for b in range(batches):
            raw(rows_of(b), 1, b, last - spot).wait_send()
            raw(w_in.at[0, b], 2, b, last - spot).wait_send()
            for slot in range(4):
                block(0, slot, b).wait()
                block(1, slot, b).wait_send()
                if slot:
                    block(2, slot, b).wait_send()
                    block(3, slot, b).wait_send()
                arrived(b, spots[slot], 1 - core)

    @pl.when(jnp.logical_not(middle))
    def _():
        for b in range(batches):
            raw(rows_of(b), 0, b, near).wait_send()
            block(0, 3, b).wait()
            block(1, 3, b).wait_send()
            arrived(b, spot, 1 - core)
            for d in range(1, ny // 2):
                for side in range(2):
                    arrived(b, lax.rem(spot + d, ny // 2), side)

    for copy in gathers:
        copy.wait()
    qo_ref[...] = q_all[...]


def exchange(w, gt, mask, q, py, nx, ny, groups, span, per_c):
    lanes = gt.shape[2]
    deep = gt.shape[1]
    z_rows = deep // ny
    dma = lambda *shape: pltpu.SemaphoreType.DMA(shape)
    vm = pltpu.VMEM
    sums = [
        vm(q.shape, F32), vm(q.shape, F32), vm((nx,) + py.shape, F32),
        vm((nx, z_rows, q.shape[2]), F32), vm((z_rows, q.shape[2]), F32),
    ]
    sum_sems = [dma(ny), dma(ny), dma(nx), dma(nx), dma(nx), dma(nx), dma(ny), dma(ny)]
    if ny == 8 and groups % 4 == 0:
        batches = 4
        per = groups // batches
        total_k = sum(
            min((t * 128 + 127) // per_c, mask.shape[0] - 1) + 1 - t * 128 // per_c
            for t in range(lanes // 128)
        ) * deep
        body = functools.partial(line_kernel, nx, ny, batches, per_c)
        scratch = [
            vm((3, batches, per * span, w.shape[1]), BF),
            vm((4, 4, batches, per, span, lanes), BF),
            vm((4, total_k, 128), BF),
        ] + sums + [
            dma(3, batches), dma(3, batches), dma(4, 4, batches), dma(batches, ny // 2, 2),
            dma(4, batches),
        ] + sum_sems
    else:
        batches = 3 if groups % 3 == 0 else 1
        per = groups // batches
        body = functools.partial(exchange_kernel, nx, ny, batches, per_c)
        scratch = [vm((batches, ny, per, span, lanes), BF)] + sums + [
            dma(batches, ny), dma(batches, ny), dma(batches)
        ] + sum_sems
    return pl.pallas_call(
        body,
        out_shape=(
            jax.ShapeDtypeStruct((groups, ny * span, lanes), BF),
            jax.ShapeDtypeStruct(q.shape, F32),
            jax.ShapeDtypeStruct(py.shape, F32),
        ),
        in_specs=[VMEM] * 5,
        out_specs=(ANY, VMEM, VMEM),
        scratch_shapes=scratch,
        compiler_params=pltpu.CompilerParams(collective_id=1, has_side_effects=True),
    )(w, gt, mask, q, py)


def mix_y_kernel(r_ref, g_ref, o_ref):
    o_ref[0] = lax.dot_general(
        r_ref[0], g_ref[...], (((0,), (0,)), ((), ())), preferred_element_type=F32
    )


def mix_y(r, g):
    groups, deep, lanes = r.shape
    out = g.shape[1]
    return pl.pallas_call(
        mix_y_kernel,
        grid=(groups,),
        out_shape=jax.ShapeDtypeStruct((groups, lanes, out), F32),
        in_specs=[
            pl.BlockSpec((1, deep, lanes), lambda i: (i, 0, 0)),
            pl.BlockSpec((deep, out), lambda i: (0, 0)),
        ],
        out_specs=pl.BlockSpec((1, lanes, out), lambda i: (i, 0, 0)),
    )(r, g)


def per_device(
    nx, ny,
    thermal_field,
    probe_range_east,
    probe_range_north,
    probe_range_upward,
    gauss_kernel_east,
    gauss_kernel_north,
    gauss_kernel_upward,
):
    rows, span, deep = thermal_field.shape
    width = probe_range_upward.shape[1]
    a_rows = gauss_kernel_east.shape[0] // nx
    per_c = gauss_kernel_upward.shape[0] // ny
    a_in = 8 if a_rows % 8 == 0 and 8 * per_c % 128 == 0 else a_rows
    groups = a_rows // a_in
    used = a_in * per_c
    lanes = -(-used // 128) * 128

    w = mix_x(
        thermal_field.reshape(rows, span * deep),
        gauss_kernel_east.reshape(nx, a_rows, -1),
        nx,
        a_rows,
    )
    w = w.reshape(groups, a_in, span, deep).transpose(0, 2, 1, 3).reshape(groups * span, a_in * deep)

    unrolled = thermal_field.reshape(rows * span, deep)
    weighted = jnp.dot(unrolled, probe_range_upward, preferred_element_type=F32)
    weighted = weighted.reshape(rows, span, width)
    along_x = probe_range_east.astype(F32)
    along_y = probe_range_north.astype(F32)
    part_x = jnp.sum(weighted * along_y[None, :, :], axis=1)
    part_y = jnp.sum(weighted * along_x[:, None, :], axis=0)
    khatri = (along_x[:, None, :] * along_y[None, :, :]).astype(BF).reshape(rows * span, width)
    part_z = lax.dot_general(
        unrolled, khatri, (((0,), (0,)), ((), ())), preferred_element_type=F32
    )
    q = jnp.concatenate(
        [part_x.reshape(ny, rows // ny, width), part_z.reshape(ny, deep // ny, width)], axis=1
    )

    gt = gauss_kernel_upward.reshape(ny, per_c, deep).transpose(0, 2, 1)
    gt = jnp.pad(jnp.tile(gt, (1, 1, a_in)), ((0, 0), (0, 0), (0, lanes - used)))
    mask = (
        lax.broadcasted_iota(jnp.int32, (a_in, lanes), 1) // per_c
        == lax.broadcasted_iota(jnp.int32, (a_in, lanes), 0)
    ).astype(BF)
    r, q_sum, factor_y = exchange(w, gt, mask, q, part_y, nx, ny, groups, span, per_c)
    factor_x = q_sum[:, : rows // ny].reshape(rows, width)
    factor_z = q_sum[:, rows // ny :].reshape(deep, width)

    core = mix_y(r, gauss_kernel_north.T)
    core = core[:, :used].reshape(a_rows, per_c, -1).transpose(0, 2, 1)
    return (factor_x, factor_y, factor_z, core)


def solution(mesh):
    in_specs = (P("gx", "gy", None), P("gx", None), P("gy", None), P(), P(), P(), P())
    out_specs = (P("gx", None), P("gy", None), P(), P("gx", None, "gy"))
    body = functools.partial(per_device, mesh.shape["gx"], mesh.shape["gy"])
    return jax.shard_map(
        body, mesh=mesh, in_specs=in_specs, out_specs=out_specs, check_vma=False
    )
```

```python
import functools

import jax
import jax.numpy as jnp
from jax import lax
from jax.experimental import pallas as pl
from jax.experimental.pallas import tpu as pltpu
from jax.sharding import PartitionSpec as P

MESH = pl.DeviceIdType.MESH
VMEM = pl.BlockSpec(memory_space=pltpu.VMEM)
ANY = pl.BlockSpec(memory_space=pl.ANY)
BF = jnp.bfloat16
F32 = jnp.float32


def remote(src, dst, send, recv, where):
    copy = pltpu.make_async_remote_copy(
        src_ref=src, dst_ref=dst, send_sem=send, recv_sem=recv, device_id=where, device_id_type=MESH
    )
    copy.start()
    return copy


def sketch_parts(f_ref, east_ref, north_ref, up_ref, q_ref, py_ref, px_buf):
    rows, span, deep = f_ref.shape
    width = up_ref.shape[1]
    step = 16 if rows % 16 == 0 else rows
    along_y = north_ref[...].astype(F32)
    part_y = jnp.zeros((span, width), F32)
    part_z = jnp.zeros((deep, width), F32)
    for c in range(0, rows, step):
        cells = f_ref[c : c + step].reshape(step * span, deep)
        along_x = east_ref[c : c + step].astype(F32)
        weighted = jnp.dot(cells, up_ref[...], preferred_element_type=F32).reshape(step, span, width)
        px_buf[c : c + step] = jnp.sum(weighted * along_y[None, :, :], axis=1)
        part_y = part_y + jnp.sum(weighted * along_x[:, None, :], axis=0)
        khatri = (along_x[:, None, :] * along_y[None, :, :]).astype(BF).reshape(step * span, width)
        part_z = part_z + lax.dot_general(
            cells, khatri, (((0,), (0,)), ((), ())), preferred_element_type=F32
        )
    py_ref[...] = part_y
    ny = q_ref.shape[0]
    x_rows, z_rows = rows // ny, deep // ny
    for k in range(ny):
        q_ref[k, :x_rows] = px_buf[k * x_rows : (k + 1) * x_rows]
        q_ref[k, x_rows:] = part_z[k * z_rows : (k + 1) * z_rows]


def mix_x_kernel(
    n, chunks, t_ref, g_ref, f_ref, east_ref, north_ref, up_ref, w_ref, q_ref, py_ref,
    x_buf, y_buf, px_buf, s1, r1, s2, r2, ls,
):
    gx, gy = lax.axis_index("gx"), lax.axis_index("gy")
    rows = t_ref.shape[0]
    a_rows = y_buf.shape[2]
    wide = t_ref.shape[1] // n
    part = wide // chunks
    barrier = pltpu.get_barrier_semaphore()
    for d in range(1, n):
        pl.semaphore_signal(barrier, inc=1, device_id=(lax.rem(gx + d, n), gy), device_id_type=MESH)
    pl.semaphore_wait(barrier, n - 1)

    first, second, local = [], [], []
    for m in range(chunks):
        for d in range(1, n):
            to = lax.rem(gx + d, n)
            lanes = pl.ds(pl.multiple_of(to * wide + m * part, 128), part)
            first.append(
                remote(t_ref.at[:, lanes], x_buf.at[m, gx], s1.at[m, d], r1.at[m, d], (to, gy))
            )
        lanes = pl.ds(pl.multiple_of(gx * wide + m * part, 128), part)
        own = pltpu.make_async_copy(t_ref.at[:, lanes], x_buf.at[m, gx], ls.at[m, 0])
        own.start()
        local.append(own)
    sketch_parts(f_ref, east_ref, north_ref, up_ref, q_ref, py_ref, px_buf)
    for m in range(chunks):
        local[m].wait()
        for d in range(1, n):
            first[m * (n - 1) + d - 1].wait()
        block = x_buf[m].reshape(n * rows, part)
        lanes = pl.ds(pl.multiple_of(gx * wide + m * part, 128), part)
        for d in range(1, n + 1):
            to = lax.rem(gx + d, n)
            y_buf[m, d - 1] = jnp.dot(g_ref[to], block, preferred_element_type=F32).astype(BF)
            if d < n:
                second.append(
                    remote(
                        y_buf.at[m, d - 1], w_ref.at[:, lanes], s2.at[m, d], r2.at[m, d], (to, gy)
                    )
                )
            else:
                own = pltpu.make_async_copy(y_buf.at[m, d - 1], w_ref.at[:, lanes], ls.at[m, 1])
                own.start()
                second.append(own)
    for copy in second:
        copy.wait()


def mix_x(field, gauss, n, a_rows, cells, east, north, up, ny):
    rows, lanes = field.shape
    wide = lanes // n
    chunks = 3 if wide % 384 == 0 else 1
    dma = lambda *shape: pltpu.SemaphoreType.DMA(shape)
    return pl.pallas_call(
        functools.partial(mix_x_kernel, n, chunks),
        out_shape=(
            jax.ShapeDtypeStruct((a_rows, lanes), BF),
            jax.ShapeDtypeStruct((ny, (cells.shape[0] + cells.shape[2]) // ny, up.shape[1]), F32),
            jax.ShapeDtypeStruct(north.shape, F32),
        ),
        in_specs=[VMEM] * 6,
        out_specs=(VMEM, VMEM, VMEM),
        scratch_shapes=[
            pltpu.VMEM((chunks, n, rows, wide // chunks), BF),
            pltpu.VMEM((chunks, n, a_rows, wide // chunks), BF),
            pltpu.VMEM(east.shape, F32),
            dma(chunks, n), dma(chunks, n), dma(chunks, n), dma(chunks, n), dma(chunks, 2),
        ],
        compiler_params=pltpu.CompilerParams(collective_id=0, has_side_effects=True),
    )(field, gauss, cells, east, north, up)


def exchange_kernel(
    nx, ny, batches, per_c, w_ref, gt_ref, mask_ref, q_ref, py_ref,
    r_ref, fx_ref, fz_ref, pyo_ref,
    u_buf, q_in, q_all, y_in, z_in, z_own,
    us, ur, ul, qs, qr, ys, yr, zs, zr, gs, gr,
):
    gx, gy = lax.axis_index("gx"), lax.axis_index("gy")
    span = u_buf.shape[3]
    per = u_buf.shape[2]
    lanes = u_buf.shape[4]
    a_in = mask_ref.shape[0]
    deep = gt_ref.shape[1]
    x_rows = q_ref.shape[1] - z_in.shape[1]
    barrier = pltpu.get_barrier_semaphore()
    for d in range(1, ny):
        pl.semaphore_signal(barrier, inc=1, device_id=(gx, lax.rem(gy + d, ny)), device_id_type=MESH)
    for d in range(1, nx):
        pl.semaphore_signal(barrier, inc=1, device_id=(lax.rem(gx + d, nx), gy), device_id_type=MESH)
    pl.semaphore_wait(barrier, nx + ny - 2)

    small, ysmall, big = [], [], []
    for d in range(1, ny):
        to = lax.rem(gy + d, ny)
        small.append(remote(q_ref.at[to], q_in.at[d], qs.at[d], qr.at[d], (gx, to)))
    for d in range(1, nx):
        to = lax.rem(gx + d, nx)
        ysmall.append(remote(py_ref, y_in.at[d], ys.at[d], yr.at[d], (to, gy)))

    rows_b = per * span
    for b in range(batches):
        for d in range(1, ny + 1):
            to = lax.rem(gy + d, ny)
            for tile in range(lanes // 128):
                low = min(tile * 128 // per_c, a_in - 1)
                high = min((tile * 128 + 127) // per_c, a_in - 1)
                here = slice(tile * 128, tile * 128 + 128)
                weights = jnp.concatenate(
                    [gt_ref[to, :, here] * mask_ref[k : k + 1, here] for k in range(low, high + 1)], axis=0
                )
                left = w_ref[b * rows_b : (b + 1) * rows_b, low * deep : (high + 1) * deep]
                got = jnp.dot(left, weights, preferred_element_type=F32).astype(BF)
                u_buf[b, d - 1, :, :, here] = got.reshape(per, span, 128)
            target = r_ref.at[pl.ds(b * per, per), pl.ds(pl.multiple_of(gy * span, span), span), :]
            if d < ny:
                big.append(remote(u_buf.at[b, d - 1], target, us.at[b, d], ur.at[b, d], (gx, to)))
            else:
                own = pltpu.make_async_copy(u_buf.at[b, d - 1], target, ul.at[b])
                own.start()
                big.append(own)
        if b == 0:
            for copy in small:
                copy.wait()
            total = q_ref[gy]
            for d in range(1, ny):
                total = total + q_in[d]
            z_own[...] = total[x_rows:]
            zsmall = []
            for d in range(1, nx):
                to = lax.rem(gx + d, nx)
                zsmall.append(remote(z_own, z_in.at[d], zs.at[d], zr.at[d], (to, gy)))
            for copy in ysmall:
                copy.wait()
            y_in[0] = py_ref[...]
            y_total = jnp.zeros(py_ref.shape, F32)
            for g in range(nx):
                y_total = y_total + y_in[lax.rem(gx - g + nx, nx)]
            pyo_ref[...] = y_total
    for copy in zsmall:
        copy.wait()
    z_in[0] = z_own[...]
    z_total = jnp.zeros(z_own.shape, F32)
    for g in range(nx):
        z_total = z_total + z_in[lax.rem(gx - g + nx, nx)]
    q_all[gy, :x_rows] = total[:x_rows]
    q_all[gy, x_rows:] = z_total
    gathers = []
    for d in range(1, ny):
        to = lax.rem(gy + d, ny)
        gathers.append(remote(q_all.at[gy], q_all.at[gy], gs.at[d], gr.at[d], (gx, to)))
    for copy in gathers:
        copy.wait()
    z_rows = z_own.shape[0]
    for k in range(ny):
        fx_ref[k * x_rows : (k + 1) * x_rows] = q_all[k, :x_rows]
        fz_ref[k * z_rows : (k + 1) * z_rows] = q_all[k, x_rows:]
    for copy in big:
        copy.wait()


def line_kernel(
    nx, ny, batches, per_c, w_ref, gt_ref, mask_ref, q_ref, py_ref,
    r_ref, fx_ref, fz_ref, pyo_ref,
    w_in, u_buf, wt, q_in, q_all, y_in, z_in, z_own,
    ws, wr, us, ur, ul, qs, qr, ys, yr, zs, zr, gs, gr,
):
    gx, gy = lax.axis_index("gx"), lax.axis_index("gy")
    spot, core = gy // 2, gy % 2
    last = ny // 2 - 1
    middle = jnp.logical_and(spot > 0, spot < last)
    left_half = spot * 2 < last
    end = jnp.where(left_half, 0, last)
    near = jnp.where(left_half, 1, last - 1)
    _, _, _, per, span, lanes = u_buf.shape
    a_in = mask_ref.shape[0]
    deep = gt_ref.shape[1]
    x_rows = q_ref.shape[1] - z_in.shape[1]
    rows_b = per * span
    spots = (end, last - spot, last - end, spot)
    goals = (gy, 2 * spot + 1 - core, 2 * end, 2 * end + 1)
    barrier = pltpu.get_barrier_semaphore()
    for d in range(1, ny):
        pl.semaphore_signal(barrier, inc=1, device_id=(gx, lax.rem(gy + d, ny)), device_id_type=MESH)
    for d in range(1, nx):
        pl.semaphore_signal(barrier, inc=1, device_id=(lax.rem(gx + d, nx), gy), device_id_type=MESH)
    pl.semaphore_wait(barrier, nx + ny - 2)

    small, ysmall = [], []
    for d in range(1, ny):
        to = lax.rem(gy + d, ny)
        small.append(remote(q_ref.at[to], q_in.at[d], qs.at[d], qr.at[d], (gx, to)))
    for d in range(1, nx):
        to = lax.rem(gx + d, nx)
        ysmall.append(remote(py_ref, y_in.at[d], ys.at[d], yr.at[d], (to, gy)))

    def raw(src, slot, b, to_spot):
        return pltpu.make_async_remote_copy(
            src_ref=src, dst_ref=w_in.at[slot, b], send_sem=ws.at[slot, b], recv_sem=wr.at[slot, b],
            device_id=(gx, 2 * to_spot + core), device_id_type=MESH,
        )

    def rows_of(b):
        return w_ref.at[pl.ds(b * rows_b, rows_b), :]

    def place(b, origin):
        return r_ref.at[pl.ds(b * per, per), pl.ds(pl.multiple_of(origin * span, span), span), :]

    def block(kind, slot, b):
        source = 2 * spots[slot] + core
        if kind == 0:
            return pltpu.make_async_copy(u_buf.at[kind, slot, b], place(b, source), ul.at[slot, b])
        return pltpu.make_async_remote_copy(
            src_ref=u_buf.at[kind, slot, b], dst_ref=place(b, source),
            send_sem=us.at[kind, slot, b], recv_sem=ur.at[b, spots[slot], core],
            device_id=(gx, goals[kind]), device_id_type=MESH,
        )

    def arrived(b, at, side):
        pltpu.make_async_remote_copy(
            src_ref=u_buf.at[0, 0, b], dst_ref=place(b, 2 * at + side),
            send_sem=us.at[1, 0, b], recv_sem=ur.at[b, at, side],
            device_id=(gx, goals[1]), device_id_type=MESH,
        ).wait_recv()

    pieces, base = [], 0
    for tile in range(lanes // 128):
        low = min(tile * 128 // per_c, a_in - 1)
        high = min((tile * 128 + 127) // per_c, a_in - 1)
        pieces.append((tile, low, high, base))
        base += (high + 1 - low) * deep

    def weigh(kind):
        for tile, low, high, at in pieces:
            here = slice(tile * 128, tile * 128 + 128)
            for k in range(low, high + 1):
                wt[kind, at + (k - low) * deep : at + (k - low + 1) * deep] = (
                    gt_ref[goals[kind], :, here] * mask_ref[k : k + 1, here]
                )

    def mix(kind, slot, b, left):
        for tile, low, high, at in pieces:
            got = jnp.dot(
                left[:, low * deep : (high + 1) * deep],
                wt[kind, at : at + (high + 1 - low) * deep],
                preferred_element_type=F32,
            ).astype(BF)
            u_buf[kind, slot, b, :, :, tile * 128 : tile * 128 + 128] = got.reshape(per, span, 128)

    def own_blocks(kind):
        weigh(kind)
        for b in range(batches):
            mix(kind, 3, b, rows_of(b))
            block(kind, 3, b).start()

    @pl.when(middle)
    def _():
        for b in range(batches):
            raw(rows_of(b), 1, b, last - spot).start()
        for kind in (2, 3):
            own_blocks(kind)

    @pl.when(jnp.logical_not(middle))
    def _():
        for b in range(batches):
            raw(rows_of(b), 0, b, near).start()

    for kind in (1, 0):
        own_blocks(kind)

    for copy in small:
        copy.wait()
    total = q_ref[gy]
    for d in range(1, ny):
        total = total + q_in[d]
    z_own[...] = total[x_rows:]
    zsmall = []
    for d in range(1, nx):
        to = lax.rem(gx + d, nx)
        zsmall.append(remote(z_own, z_in.at[d], zs.at[d], zr.at[d], (to, gy)))
    for copy in ysmall:
        copy.wait()
    y_in[0] = py_ref[...]
    y_total = jnp.zeros(py_ref.shape, F32)
    for g in range(nx):
        y_total = y_total + y_in[lax.rem(gx - g + nx, nx)]
    pyo_ref[...] = y_total
    for copy in zsmall:
        copy.wait()
    z_in[0] = z_own[...]
    z_total = jnp.zeros(z_own.shape, F32)
    for g in range(nx):
        z_total = z_total + z_in[lax.rem(gx - g + nx, nx)]
    q_all[gy, :x_rows] = total[:x_rows]
    q_all[gy, x_rows:] = z_total
    gathers = []
    for d in range(1, ny):
        to = lax.rem(gy + d, ny)
        gathers.append(remote(q_all.at[gy], q_all.at[gy], gs.at[d], gr.at[d], (gx, to)))

    @pl.when(middle)
    def _():
        for b in range(batches):
            raw(rows_of(b), 0, b, near).wait_recv()
            raw(w_in.at[0, b], 2, b, last - spot).start()
            raw(rows_of(b), 1, b, last - spot).wait_recv()
            for kind, slot in ((2, 1), (3, 1), (1, 1), (1, 0), (0, 1), (0, 0)):
                mix(kind, slot, b, w_in.at[slot, b])
                block(kind, slot, b).start()
        for b in range(batches):
            raw(w_in.at[0, b], 2, b, last - spot).wait_recv()
            for kind in (2, 3, 1, 0):
                mix(kind, 2, b, w_in.at[2, b])
                block(kind, 2, b).start()
        for b in range(batches):
            raw(rows_of(b), 1, b, last - spot).wait_send()
            raw(w_in.at[0, b], 2, b, last - spot).wait_send()
            for slot in range(4):
                block(0, slot, b).wait()
                block(1, slot, b).wait_send()
                if slot:
                    block(2, slot, b).wait_send()
                    block(3, slot, b).wait_send()
                arrived(b, spots[slot], 1 - core)

    @pl.when(jnp.logical_not(middle))
    def _():
        for b in range(batches):
            raw(rows_of(b), 0, b, near).wait_send()
            block(0, 3, b).wait()
            block(1, 3, b).wait_send()
            arrived(b, spot, 1 - core)
            for d in range(1, ny // 2):
                for side in range(2):
                    arrived(b, lax.rem(spot + d, ny // 2), side)

    for copy in gathers:
        copy.wait()
    z_rows = z_own.shape[0]
    for k in range(ny):
        fx_ref[k * x_rows : (k + 1) * x_rows] = q_all[k, :x_rows]
        fz_ref[k * z_rows : (k + 1) * z_rows] = q_all[k, x_rows:]


def exchange(w, gt, mask, q, py, nx, ny, groups, span, per_c):
    lanes = gt.shape[2]
    deep = gt.shape[1]
    z_rows = deep // ny
    dma = lambda *shape: pltpu.SemaphoreType.DMA(shape)
    vm = pltpu.VMEM
    sums = [
        vm(q.shape, F32), vm(q.shape, F32), vm((nx,) + py.shape, F32),
        vm((nx, z_rows, q.shape[2]), F32), vm((z_rows, q.shape[2]), F32),
    ]
    sum_sems = [dma(ny), dma(ny), dma(nx), dma(nx), dma(nx), dma(nx), dma(ny), dma(ny)]
    if ny == 8 and groups % 4 == 0:
        batches = 4
        per = groups // batches
        total_k = sum(
            min((t * 128 + 127) // per_c, mask.shape[0] - 1) + 1 - t * 128 // per_c
            for t in range(lanes // 128)
        ) * deep
        body = functools.partial(line_kernel, nx, ny, batches, per_c)
        scratch = [
            vm((3, batches, per * span, w.shape[1]), BF),
            vm((4, 4, batches, per, span, lanes), BF),
            vm((4, total_k, 128), BF),
        ] + sums + [
            dma(3, batches), dma(3, batches), dma(4, 4, batches), dma(batches, ny // 2, 2),
            dma(4, batches),
        ] + sum_sems
    else:
        batches = 3 if groups % 3 == 0 else 1
        per = groups // batches
        body = functools.partial(exchange_kernel, nx, ny, batches, per_c)
        scratch = [vm((batches, ny, per, span, lanes), BF)] + sums + [
            dma(batches, ny), dma(batches, ny), dma(batches)
        ] + sum_sems
    return pl.pallas_call(
        body,
        out_shape=(
            jax.ShapeDtypeStruct((groups, ny * span, lanes), BF),
            jax.ShapeDtypeStruct((ny * q.shape[1] - deep, q.shape[2]), F32),
            jax.ShapeDtypeStruct((deep, q.shape[2]), F32),
            jax.ShapeDtypeStruct(py.shape, F32),
        ),
        in_specs=[VMEM] * 5,
        out_specs=(ANY, VMEM, VMEM, VMEM),
        scratch_shapes=scratch,
        compiler_params=pltpu.CompilerParams(collective_id=1, has_side_effects=True),
    )(w, gt, mask, q, py)


def mix_y_kernel(r_ref, g_ref, o_ref):
    for k in range(r_ref.shape[0]):
        o_ref[k] = lax.dot_general(
            r_ref[k], g_ref[...], (((0,), (0,)), ((), ())), preferred_element_type=F32
        )


def mix_y(r, g):
    groups, deep, lanes = r.shape
    out = g.shape[1]
    take = 2 if groups % 2 == 0 else 1
    return pl.pallas_call(
        mix_y_kernel,
        grid=(groups // take,),
        out_shape=jax.ShapeDtypeStruct((groups, lanes, out), F32),
        in_specs=[
            pl.BlockSpec((take, deep, lanes), lambda i: (i, 0, 0)),
            pl.BlockSpec((deep, out), lambda i: (0, 0)),
        ],
        out_specs=pl.BlockSpec((take, lanes, out), lambda i: (i, 0, 0)),
    )(r, g)


def per_device(
    nx, ny,
    thermal_field,
    probe_range_east,
    probe_range_north,
    probe_range_upward,
    gauss_kernel_east,
    gauss_kernel_north,
    gauss_kernel_upward,
):
    rows, span, deep = thermal_field.shape
    a_rows = gauss_kernel_east.shape[0] // nx
    per_c = gauss_kernel_upward.shape[0] // ny
    a_in = 8 if a_rows % 8 == 0 and 8 * per_c % 128 == 0 else a_rows
    groups = a_rows // a_in
    used = a_in * per_c
    lanes = -(-used // 128) * 128

    w, q, part_y = mix_x(
        thermal_field.reshape(rows, span * deep),
        gauss_kernel_east.reshape(nx, a_rows, -1),
        nx,
        a_rows,
        thermal_field,
        probe_range_east,
        probe_range_north,
        probe_range_upward,
        ny,
    )
    w = w.reshape(groups, a_in, span, deep).transpose(0, 2, 1, 3).reshape(groups * span, a_in * deep)

    gt = gauss_kernel_upward.reshape(ny, per_c, deep).transpose(0, 2, 1)
    gt = jnp.pad(jnp.tile(gt, (1, 1, a_in)), ((0, 0), (0, 0), (0, lanes - used)))
    mask = (
        lax.broadcasted_iota(jnp.int32, (a_in, lanes), 1) // per_c
        == lax.broadcasted_iota(jnp.int32, (a_in, lanes), 0)
    ).astype(BF)
    r, factor_x, factor_z, factor_y = exchange(w, gt, mask, q, part_y, nx, ny, groups, span, per_c)

    core = mix_y(r, gauss_kernel_north.T)
    core = core[:, :used].reshape(a_rows, per_c, -1).transpose(0, 2, 1)
    return (factor_x, factor_y, factor_z, core)


def solution(mesh):
    in_specs = (P("gx", "gy", None), P("gx", None), P("gy", None), P(), P(), P(), P())
    out_specs = (P("gx", None), P("gy", None), P(), P("gx", None, "gy"))
    body = functools.partial(per_device, mesh.shape["gx"], mesh.shape["gy"])
    return jax.shard_map(
        body, mesh=mesh, in_specs=in_specs, out_specs=out_specs, check_vma=False
    )
```

```python
import functools

import jax
import jax.numpy as jnp
from jax import lax
from jax.experimental import pallas as pl
from jax.experimental.pallas import tpu as pltpu
from jax.sharding import PartitionSpec as P

MESH = pl.DeviceIdType.MESH
VMEM = pl.BlockSpec(memory_space=pltpu.VMEM)
ANY = pl.BlockSpec(memory_space=pl.ANY)
BF = jnp.bfloat16
F32 = jnp.float32


def remote(src, dst, send, recv, where):
    copy = pltpu.make_async_remote_copy(
        src_ref=src, dst_ref=dst, send_sem=send, recv_sem=recv, device_id=where, device_id_type=MESH
    )
    copy.start()
    return copy


def sketch_parts(f_ref, east_ref, north_ref, up_ref, q_ref, py_ref, px_buf):
    rows, span, deep = f_ref.shape
    width = up_ref.shape[1]
    step = 16 if rows % 16 == 0 else rows
    along_y = north_ref[...].astype(F32)
    part_y = jnp.zeros((span, width), F32)
    part_z = jnp.zeros((deep, width), F32)
    for c in range(0, rows, step):
        cells = f_ref[c : c + step].reshape(step * span, deep)
        along_x = east_ref[c : c + step].astype(F32)
        weighted = jnp.dot(cells, up_ref[...], preferred_element_type=F32).reshape(step, span, width)
        px_buf[c : c + step] = jnp.sum(weighted * along_y[None, :, :], axis=1)
        part_y = part_y + jnp.sum(weighted * along_x[:, None, :], axis=0)
        khatri = (along_x[:, None, :] * along_y[None, :, :]).astype(BF).reshape(step * span, width)
        part_z = part_z + lax.dot_general(
            cells, khatri, (((0,), (0,)), ((), ())), preferred_element_type=F32
        )
    py_ref[...] = part_y
    ny = q_ref.shape[0]
    x_rows, z_rows = rows // ny, deep // ny
    for k in range(ny):
        q_ref[k, :x_rows] = px_buf[k * x_rows : (k + 1) * x_rows]
        q_ref[k, x_rows:] = part_z[k * z_rows : (k + 1) * z_rows]


def mix_x_kernel(
    n, chunks, t_ref, g_ref, f_ref, east_ref, north_ref, up_ref, w_ref, q_ref, py_ref,
    x_buf, y_buf, px_buf, s1, r1, s2, r2, ls,
):
    gx, gy = lax.axis_index("gx"), lax.axis_index("gy")
    rows = t_ref.shape[0]
    a_rows = y_buf.shape[2]
    wide = t_ref.shape[1] // n
    part = wide // chunks
    barrier = pltpu.get_barrier_semaphore()
    for d in range(1, n):
        pl.semaphore_signal(barrier, inc=1, device_id=(lax.rem(gx + d, n), gy), device_id_type=MESH)
    pl.semaphore_wait(barrier, n - 1)

    first, second, local = [], [], []
    for m in range(chunks):
        for d in range(1, n):
            to = lax.rem(gx + d, n)
            lanes = pl.ds(pl.multiple_of(to * wide + m * part, 128), part)
            first.append(
                remote(t_ref.at[:, lanes], x_buf.at[m, gx], s1.at[m, d], r1.at[m, d], (to, gy))
            )
        lanes = pl.ds(pl.multiple_of(gx * wide + m * part, 128), part)
        own = pltpu.make_async_copy(t_ref.at[:, lanes], x_buf.at[m, gx], ls.at[m, 0])
        own.start()
        local.append(own)
    sketch_parts(f_ref, east_ref, north_ref, up_ref, q_ref, py_ref, px_buf)
    for m in range(chunks):
        local[m].wait()
        for d in range(1, n):
            first[m * (n - 1) + d - 1].wait()
        block = x_buf[m].reshape(n * rows, part)
        lanes = pl.ds(pl.multiple_of(gx * wide + m * part, 128), part)
        for d in range(1, n + 1):
            to = lax.rem(gx + d, n)
            y_buf[m, d - 1] = jnp.dot(g_ref[to], block, preferred_element_type=F32).astype(BF)
            if d < n:
                second.append(
                    remote(
                        y_buf.at[m, d - 1], w_ref.at[:, lanes], s2.at[m, d], r2.at[m, d], (to, gy)
                    )
                )
            else:
                own = pltpu.make_async_copy(y_buf.at[m, d - 1], w_ref.at[:, lanes], ls.at[m, 1])
                own.start()
                second.append(own)
    for copy in second:
        copy.wait()


def mix_x(field, gauss, n, a_rows, cells, east, north, up, ny):
    rows, lanes = field.shape
    wide = lanes // n
    chunks = 3 if wide % 384 == 0 else 1
    dma = lambda *shape: pltpu.SemaphoreType.DMA(shape)
    return pl.pallas_call(
        functools.partial(mix_x_kernel, n, chunks),
        out_shape=(
            jax.ShapeDtypeStruct((a_rows, lanes), BF),
            jax.ShapeDtypeStruct((ny, (cells.shape[0] + cells.shape[2]) // ny, up.shape[1]), F32),
            jax.ShapeDtypeStruct(north.shape, F32),
        ),
        in_specs=[VMEM] * 6,
        out_specs=(VMEM, VMEM, VMEM),
        scratch_shapes=[
            pltpu.VMEM((chunks, n, rows, wide // chunks), BF),
            pltpu.VMEM((chunks, n, a_rows, wide // chunks), BF),
            pltpu.VMEM(east.shape, F32),
            dma(chunks, n), dma(chunks, n), dma(chunks, n), dma(chunks, n), dma(chunks, 2),
        ],
        compiler_params=pltpu.CompilerParams(collective_id=0, has_side_effects=True),
    )(field, gauss, cells, east, north, up)


def exchange_kernel(
    nx, ny, batches, per_c, w_ref, gt_ref, mask_ref, q_ref, py_ref,
    r_ref, fx_ref, fz_ref, pyo_ref,
    u_buf, q_in, q_all, y_in, z_in, z_own,
    us, ur, ul, qs, qr, ys, yr, zs, zr, gs, gr,
):
    gx, gy = lax.axis_index("gx"), lax.axis_index("gy")
    span = u_buf.shape[3]
    per = u_buf.shape[2]
    lanes = u_buf.shape[4]
    a_in = mask_ref.shape[0]
    deep = gt_ref.shape[1]
    x_rows = q_ref.shape[1] - z_in.shape[1]
    barrier = pltpu.get_barrier_semaphore()
    for d in range(1, ny):
        pl.semaphore_signal(barrier, inc=1, device_id=(gx, lax.rem(gy + d, ny)), device_id_type=MESH)
    for d in range(1, nx):
        pl.semaphore_signal(barrier, inc=1, device_id=(lax.rem(gx + d, nx), gy), device_id_type=MESH)
    pl.semaphore_wait(barrier, nx + ny - 2)

    small, ysmall, big = [], [], []
    for d in range(1, ny):
        to = lax.rem(gy + d, ny)
        small.append(remote(q_ref.at[to], q_in.at[d], qs.at[d], qr.at[d], (gx, to)))
    for d in range(1, nx):
        to = lax.rem(gx + d, nx)
        ysmall.append(remote(py_ref, y_in.at[d], ys.at[d], yr.at[d], (to, gy)))

    rows_b = per * span
    for b in range(batches):
        for d in range(1, ny + 1):
            to = lax.rem(gy + d, ny)
            for tile in range(lanes // 128):
                low = min(tile * 128 // per_c, a_in - 1)
                high = min((tile * 128 + 127) // per_c, a_in - 1)
                here = slice(tile * 128, tile * 128 + 128)
                weights = jnp.concatenate(
                    [gt_ref[to, :, here] * mask_ref[k : k + 1, here] for k in range(low, high + 1)], axis=0
                )
                left = w_ref[b * rows_b : (b + 1) * rows_b, low * deep : (high + 1) * deep]
                got = jnp.dot(left, weights, preferred_element_type=F32).astype(BF)
                u_buf[b, d - 1, :, :, here] = got.reshape(per, span, 128)
            target = r_ref.at[pl.ds(b * per, per), pl.ds(pl.multiple_of(gy * span, span), span), :]
            if d < ny:
                big.append(remote(u_buf.at[b, d - 1], target, us.at[b, d], ur.at[b, d], (gx, to)))
            else:
                own = pltpu.make_async_copy(u_buf.at[b, d - 1], target, ul.at[b])
                own.start()
                big.append(own)
        if b == 0:
            for copy in small:
                copy.wait()
            total = q_ref[gy]
            for d in range(1, ny):
                total = total + q_in[d]
            z_own[...] = total[x_rows:]
            zsmall = []
            for d in range(1, nx):
                to = lax.rem(gx + d, nx)
                zsmall.append(remote(z_own, z_in.at[d], zs.at[d], zr.at[d], (to, gy)))
            for copy in ysmall:
                copy.wait()
            y_in[0] = py_ref[...]
            y_total = jnp.zeros(py_ref.shape, F32)
            for g in range(nx):
                y_total = y_total + y_in[lax.rem(gx - g + nx, nx)]
            pyo_ref[...] = y_total
    for copy in zsmall:
        copy.wait()
    z_in[0] = z_own[...]
    z_total = jnp.zeros(z_own.shape, F32)
    for g in range(nx):
        z_total = z_total + z_in[lax.rem(gx - g + nx, nx)]
    q_all[gy, :x_rows] = total[:x_rows]
    q_all[gy, x_rows:] = z_total
    gathers = []
    for d in range(1, ny):
        to = lax.rem(gy + d, ny)
        gathers.append(remote(q_all.at[gy], q_all.at[gy], gs.at[d], gr.at[d], (gx, to)))
    for copy in gathers:
        copy.wait()
    z_rows = z_own.shape[0]
    for k in range(ny):
        fx_ref[k * x_rows : (k + 1) * x_rows] = q_all[k, :x_rows]
        fz_ref[k * z_rows : (k + 1) * z_rows] = q_all[k, x_rows:]
    for copy in big:
        copy.wait()


def line_kernel(
    nx, ny, batches, per_c, w_ref, gt_ref, mask_ref, q_ref, py_ref,
    r_ref, fx_ref, fz_ref, pyo_ref,
    w_in, u_buf, wt, q_in, q_all, y_in, z_in, z_own,
    ws, wr, us, ur, ul, qs, qr, ys, yr, zs, zr, gs, gr,
):
    gx, gy = lax.axis_index("gx"), lax.axis_index("gy")
    spot, core = gy // 2, gy % 2
    last = ny // 2 - 1
    middle = jnp.logical_and(spot > 0, spot < last)
    left_half = spot * 2 < last
    end = jnp.where(left_half, 0, last)
    near = jnp.where(left_half, 1, last - 1)
    _, _, _, per, span, lanes = u_buf.shape
    a_in = mask_ref.shape[0]
    deep = gt_ref.shape[1]
    x_rows = q_ref.shape[1] - z_in.shape[1]
    rows_b = per * span
    spots = (end, last - spot, last - end, spot)
    goals = (gy, 2 * spot + 1 - core, 2 * end, 2 * end + 1)
    barrier = pltpu.get_barrier_semaphore()
    for d in range(1, ny):
        pl.semaphore_signal(barrier, inc=1, device_id=(gx, lax.rem(gy + d, ny)), device_id_type=MESH)
    for d in range(1, nx):
        pl.semaphore_signal(barrier, inc=1, device_id=(lax.rem(gx + d, nx), gy), device_id_type=MESH)
    pl.semaphore_wait(barrier, nx + ny - 2)

    small, ysmall = [], []
    for d in range(1, ny):
        to = lax.rem(gy + d, ny)
        small.append(remote(q_ref.at[to], q_in.at[d], qs.at[d], qr.at[d], (gx, to)))
    for d in range(1, nx):
        to = lax.rem(gx + d, nx)
        ysmall.append(remote(py_ref, y_in.at[d], ys.at[d], yr.at[d], (to, gy)))

    def raw(src, slot, b, to_spot):
        return pltpu.make_async_remote_copy(
            src_ref=src, dst_ref=w_in.at[slot, b], send_sem=ws.at[slot, b], recv_sem=wr.at[slot, b],
            device_id=(gx, 2 * to_spot + core), device_id_type=MESH,
        )

    def rows_of(b):
        return w_ref.at[pl.ds(b * rows_b, rows_b), :]

    def place(b, origin):
        return r_ref.at[pl.ds(b * per, per), pl.ds(pl.multiple_of(origin * span, span), span), :]

    def block(kind, slot, b):
        source = 2 * spots[slot] + core
        if kind == 0:
            return pltpu.make_async_copy(u_buf.at[kind, slot, b], place(b, source), ul.at[slot, b])
        return pltpu.make_async_remote_copy(
            src_ref=u_buf.at[kind, slot, b], dst_ref=place(b, source),
            send_sem=us.at[kind, slot, b], recv_sem=ur.at[b, spots[slot], core],
            device_id=(gx, goals[kind]), device_id_type=MESH,
        )

    def arrived(b, at, side):
        pltpu.make_async_remote_copy(
            src_ref=u_buf.at[0, 0, b], dst_ref=place(b, 2 * at + side),
            send_sem=us.at[1, 0, b], recv_sem=ur.at[b, at, side],
            device_id=(gx, goals[1]), device_id_type=MESH,
        ).wait_recv()

    pieces, base = [], 0
    for tile in range(lanes // 128):
        low = min(tile * 128 // per_c, a_in - 1)
        high = min((tile * 128 + 127) // per_c, a_in - 1)
        pieces.append((tile, low, high, base))
        base += (high + 1 - low) * deep

    def weigh(kind):
        for tile, low, high, at in pieces:
            here = slice(tile * 128, tile * 128 + 128)
            for k in range(low, high + 1):
                wt[kind, at + (k - low) * deep : at + (k - low + 1) * deep] = (
                    gt_ref[goals[kind], :, here] * mask_ref[k : k + 1, here]
                )

    def mix(kind, slot, b, left):
        for tile, low, high, at in pieces:
            got = jnp.dot(
                left[:, low * deep : (high + 1) * deep],
                wt[kind, at : at + (high + 1 - low) * deep],
                preferred_element_type=F32,
            ).astype(BF)
            u_buf[kind, slot, b, :, :, tile * 128 : tile * 128 + 128] = got.reshape(per, span, 128)

    def own_blocks(kind):
        weigh(kind)
        for b in range(batches):
            mix(kind, 3, b, rows_of(b))
            block(kind, 3, b).start()

    @pl.when(middle)
    def _():
        for b in range(batches):
            raw(rows_of(b), 1, b, last - spot).start()
        for kind in (2, 3):
            own_blocks(kind)

    @pl.when(jnp.logical_not(middle))
    def _():
        for b in range(batches):
            raw(rows_of(b), 0, b, near).start()

    for kind in (1, 0):
        own_blocks(kind)

    for copy in small:
        copy.wait()
    total = q_ref[gy]
    for d in range(1, ny):
        total = total + q_in[d]
    z_own[...] = total[x_rows:]
    zsmall = []
    for d in range(1, nx):
        to = lax.rem(gx + d, nx)
        zsmall.append(remote(z_own, z_in.at[d], zs.at[d], zr.at[d], (to, gy)))
    for copy in ysmall:
        copy.wait()
    y_in[0] = py_ref[...]
    y_total = jnp.zeros(py_ref.shape, F32)
    for g in range(nx):
        y_total = y_total + y_in[lax.rem(gx - g + nx, nx)]
    pyo_ref[...] = y_total
    for copy in zsmall:
        copy.wait()
    z_in[0] = z_own[...]
    z_total = jnp.zeros(z_own.shape, F32)
    for g in range(nx):
        z_total = z_total + z_in[lax.rem(gx - g + nx, nx)]
    q_all[gy, :x_rows] = total[:x_rows]
    q_all[gy, x_rows:] = z_total
    gathers = []
    for d in range(1, ny):
        to = lax.rem(gy + d, ny)
        gathers.append(remote(q_all.at[gy], q_all.at[gy], gs.at[d], gr.at[d], (gx, to)))

    @pl.when(middle)
    def _():
        for b in range(batches):
            raw(rows_of(b), 0, b, near).wait_recv()
            raw(w_in.at[0, b], 2, b, last - spot).start()
            raw(rows_of(b), 1, b, last - spot).wait_recv()
            for kind, slot in ((2, 1), (3, 1), (1, 1), (1, 0), (0, 1), (0, 0)):
                mix(kind, slot, b, w_in.at[slot, b])
                block(kind, slot, b).start()
        for b in range(batches):
            raw(w_in.at[0, b], 2, b, last - spot).wait_recv()
            for kind in (2, 3, 1, 0):
                mix(kind, 2, b, w_in.at[2, b])
                block(kind, 2, b).start()
        for b in range(batches):
            raw(rows_of(b), 1, b, last - spot).wait_send()
            raw(w_in.at[0, b], 2, b, last - spot).wait_send()
            for slot in range(4):
                block(0, slot, b).wait()
                block(1, slot, b).wait_send()
                if slot:
                    block(2, slot, b).wait_send()
                    block(3, slot, b).wait_send()
                arrived(b, spots[slot], 1 - core)

    @pl.when(jnp.logical_not(middle))
    def _():
        for b in range(batches):
            raw(rows_of(b), 0, b, near).wait_send()
            block(0, 3, b).wait()
            block(1, 3, b).wait_send()
            arrived(b, spot, 1 - core)
            for d in range(1, ny // 2):
                for side in range(2):
                    arrived(b, lax.rem(spot + d, ny // 2), side)

    for copy in gathers:
        copy.wait()
    z_rows = z_own.shape[0]
    for k in range(ny):
        fx_ref[k * x_rows : (k + 1) * x_rows] = q_all[k, :x_rows]
        fz_ref[k * z_rows : (k + 1) * z_rows] = q_all[k, x_rows:]


def exchange(w, gt, mask, q, py, nx, ny, groups, span, per_c):
    lanes = gt.shape[2]
    deep = gt.shape[1]
    z_rows = deep // ny
    dma = lambda *shape: pltpu.SemaphoreType.DMA(shape)
    vm = pltpu.VMEM
    sums = [
        vm(q.shape, F32), vm(q.shape, F32), vm((nx,) + py.shape, F32),
        vm((nx, z_rows, q.shape[2]), F32), vm((z_rows, q.shape[2]), F32),
    ]
    sum_sems = [dma(ny), dma(ny), dma(nx), dma(nx), dma(nx), dma(nx), dma(ny), dma(ny)]
    if ny == 8 and groups % 4 == 0:
        batches = 4
        per = groups // batches
        total_k = sum(
            min((t * 128 + 127) // per_c, mask.shape[0] - 1) + 1 - t * 128 // per_c
            for t in range(lanes // 128)
        ) * deep
        body = functools.partial(line_kernel, nx, ny, batches, per_c)
        scratch = [
            vm((3, batches, per * span, w.shape[1]), BF),
            vm((4, 4, batches, per, span, lanes), BF),
            vm((4, total_k, 128), BF),
        ] + sums + [
            dma(3, batches), dma(3, batches), dma(4, 4, batches), dma(batches, ny // 2, 2),
            dma(4, batches),
        ] + sum_sems
    else:
        batches = 3 if groups % 3 == 0 else 1
        per = groups // batches
        body = functools.partial(exchange_kernel, nx, ny, batches, per_c)
        scratch = [vm((batches, ny, per, span, lanes), BF)] + sums + [
            dma(batches, ny), dma(batches, ny), dma(batches)
        ] + sum_sems
    return pl.pallas_call(
        body,
        out_shape=(
            jax.ShapeDtypeStruct((groups, ny * span, lanes), BF),
            jax.ShapeDtypeStruct((ny * q.shape[1] - deep, q.shape[2]), F32),
            jax.ShapeDtypeStruct((deep, q.shape[2]), F32),
            jax.ShapeDtypeStruct(py.shape, F32),
        ),
        in_specs=[VMEM] * 5,
        out_specs=(ANY, VMEM, VMEM, VMEM),
        scratch_shapes=scratch,
        compiler_params=pltpu.CompilerParams(collective_id=1, has_side_effects=True),
    )(w, gt, mask, q, py)


def mix_y_kernel(r_ref, g_ref, o_ref):
    for k in range(r_ref.shape[0]):
        o_ref[k] = lax.dot_general(
            r_ref[k], g_ref[...], (((0,), (1,)), ((), ())), preferred_element_type=F32
        )


def mix_y(r, g):
    groups, deep, lanes = r.shape
    out = g.shape[0]
    take = 2 if groups % 2 == 0 else 1
    return pl.pallas_call(
        mix_y_kernel,
        grid=(groups // take,),
        out_shape=jax.ShapeDtypeStruct((groups, lanes, out), F32),
        in_specs=[
            pl.BlockSpec((take, deep, lanes), lambda i: (i, 0, 0)),
            pl.BlockSpec((out, deep), lambda i: (0, 0)),
        ],
        out_specs=pl.BlockSpec((take, lanes, out), lambda i: (i, 0, 0)),
    )(r, g)


def per_device(
    nx, ny,
    thermal_field,
    probe_range_east,
    probe_range_north,
    probe_range_upward,
    gauss_kernel_east,
    gauss_kernel_north,
    gauss_kernel_upward,
):
    rows, span, deep = thermal_field.shape
    a_rows = gauss_kernel_east.shape[0] // nx
    per_c = gauss_kernel_upward.shape[0] // ny
    a_in = 8 if a_rows % 8 == 0 and 8 * per_c % 128 == 0 else a_rows
    groups = a_rows // a_in
    used = a_in * per_c
    lanes = -(-used // 128) * 128

    w, q, part_y = mix_x(
        thermal_field.reshape(rows, span * deep),
        gauss_kernel_east.reshape(nx, a_rows, -1),
        nx,
        a_rows,
        thermal_field,
        probe_range_east,
        probe_range_north,
        probe_range_upward,
        ny,
    )
    w = w.reshape(groups, a_in, span, deep).transpose(0, 2, 1, 3).reshape(groups * span, a_in * deep)

    gt = gauss_kernel_upward.reshape(ny, per_c, deep).transpose(0, 2, 1)
    gt = jnp.pad(jnp.tile(gt, (1, 1, a_in)), ((0, 0), (0, 0), (0, lanes - used)))
    mask = (
        lax.broadcasted_iota(jnp.int32, (a_in, lanes), 1) // per_c
        == lax.broadcasted_iota(jnp.int32, (a_in, lanes), 0)
    ).astype(BF)
    r, factor_x, factor_z, factor_y = exchange(w, gt, mask, q, part_y, nx, ny, groups, span, per_c)

    core = mix_y(r, gauss_kernel_north)
    core = core[:, :used].reshape(a_rows, per_c, -1).transpose(0, 2, 1)
    return (factor_x, factor_y, factor_z, core)


def solution(mesh):
    in_specs = (P("gx", "gy", None), P("gx", None), P("gy", None), P(), P(), P(), P())
    out_specs = (P("gx", None), P("gy", None), P(), P("gx", None, "gy"))
    body = functools.partial(per_device, mesh.shape["gx"], mesh.shape["gy"])
    return jax.shard_map(
        body, mesh=mesh, in_specs=in_specs, out_specs=out_specs, check_vma=False
    )
```
